32 devices in a mesh: row: 2 (over x), col: 16 (over z, y, core).
Axes of the slice: x: 2, y: 2, z: 4, core: 2. Of those that a mesh axis runs over, the one named last changes fastest.
Arguments:
- activations: bfloat16 [128, 8192], P('col', 'row'), may hold values from -6 to 6
- up_weight: bfloat16 [8192, 53248], P('row', 'col'), may hold values from -0.0625 to 0.0625
- out_grad: bfloat16 [128, 53248], P('row', 'col'), may hold values from -6 to 6
- round_seed: int32 [1], replicated, may hold values from 0 to 1073741823
- counter_base: int32 [128], P('row'), may hold values from 0 to 1073741823
Outputs:
- weight_grad: float32 [8192, 53248], P('row', 'col')
- input_grad: bfloat16 [128, 8192], P('col', 'row')
The draws below stay inside these ranges and needn't reach their ends.
All inputs are finite; a program needn't handle non-finite values.
Results may differ from the reference program's by a relative error of at most 0.015.
Values may be sent and summed in bfloat16 or wider, within the bound.
No kernel may reach another device: no remote copies, remote signals or barrier semaphores. Data moves between devices by JAX's collectives and lax.ppermute only.
A program may use at most 192 MiB of HBM per device.

```python
import jax
import jax.numpy as jnp
from jax import lax

D = 8192
FF = 53248
TOKENS = 128
FF_BLOCK = 3328
N_COL = 16


def touch_ends(drawn, key, least, largest):
    longest = drawn.shape.index(max(drawn.shape))
    spots = []
    for shift in (0, 1):
        where = [jax.random.randint(jax.random.fold_in(key, axis), (), 0, length) for axis, length in enumerate(drawn.shape)]
        where[longest] = (where[longest] + shift) % drawn.shape[longest]
        spots.append(tuple(where))
    return drawn.at[spots[0]].set(least).at[spots[1]].set(largest)


def level_of(own_key, shape, split, smallest, largest):
    factor_of = 1.0
    for position, blocks in split:
        steps = jax.random.uniform(jax.random.fold_in(jax.random.fold_in(own_key, 6), position), (blocks,), jnp.float32, smallest / len(split), largest / len(split))
        factor_of = factor_of * jnp.repeat(jnp.exp(steps), shape[position] // blocks).reshape((-1,) + (1,) * (len(shape) - 1 - position))
    return factor_of


def noise(stream_key, extent, deviation, most, shards=(), kind=jnp.bfloat16):
    values = deviation * jax.random.normal(stream_key, extent, jnp.float32)
    if shards:
        values = values * level_of(stream_key, extent, shards, -0.22, 0.18)
    return jnp.clip(values, -most, most).astype(kind)


def setup_inputs(seed: int = 0) -> dict:
    key_list = jax.random.split(jax.random.key(seed), 6)
    return {
        "activations": noise(key_list[0], (TOKENS, D), 1.0, 6.0, ((0, 16), (1, 2))),
        "up_weight": noise(key_list[1], (D, FF), D ** -0.5, 0.0625, ((0, 2), (1, 16))),
        "out_grad": noise(key_list[2], (TOKENS, FF), 1.0, 6.0, ((0, 2), (1, 16))),
        "round_seed": jax.random.randint(key_list[3], (1,), 0, 1073741824).astype(jnp.int32),
        "counter_base": touch_ends(jax.random.randint(key_list[4], (TOKENS,), 0, 1073741824), jax.random.fold_in(key_list[4], 1), 0, 1073741823).astype(jnp.int32),
    }


def stochastic_round(grad, counter_base, round_seed, col_first):
    columns = col_first + lax.broadcasted_iota(jnp.int32, grad.shape, 1)
    counter = counter_base[:, None] + columns
    mixed = counter * jnp.int32(747796405) + round_seed[0] * jnp.int32(1013904223)
    mixed = mixed ^ (mixed >> 15)
    mixed = mixed * jnp.int32(277803737)
    mixed = mixed ^ (mixed >> 16)
    level = (mixed & 255).astype(jnp.float32)
    scaled = grad.astype(jnp.float32) * 4.0 + (level + 0.5) / 256.0
    return (jnp.floor(scaled) / 4.0).astype(jnp.bfloat16)


def reference(activations, up_weight, out_grad, round_seed, counter_base):
    quantized = stochastic_round(out_grad, counter_base, round_seed, 0)
    weight_grad = jnp.dot(activations.T, quantized, preferred_element_type=jnp.float32) * (TOKENS ** -0.5)

    def add_block(block, total):
        offset = (block * FF_BLOCK).astype(jnp.int32)
        grad_rows = lax.dynamic_slice_in_dim(quantized, offset, FF_BLOCK, 1)
        weight_cols = lax.dynamic_slice_in_dim(up_weight, offset, FF_BLOCK, 1)
        partial_value = jnp.dot(grad_rows, weight_cols.T, preferred_element_type=jnp.float32).astype(jnp.bfloat16)
        partial_value = lax.optimization_barrier(partial_value)
        return total + partial_value.astype(jnp.float32)

    summed = lax.fori_loop(0, N_COL, add_block, jnp.zeros((TOKENS, D), jnp.float32))
    return weight_grad, summed.astype(jnp.bfloat16)
```

```python
import functools

import jax
import jax.numpy as jnp
from jax import lax
from jax.experimental import pallas as pl
from jax.experimental.pallas import tpu as pltpu
from jax.sharding import PartitionSpec as P


CORES = 2
MIB = 2**20


def round_kernel(per_col, seed_ref, base_ref, grad_ref, out_ref):
    rows, f_local = grad_ref.shape
    shape = (rows, rows)
    diagonal = lax.broadcasted_iota(jnp.int32, shape, 0) == lax.broadcasted_iota(
        jnp.int32, shape, 1
    )
    base = jnp.where(diagonal, jnp.broadcast_to(base_ref[...], shape), 0)
    base = jnp.sum(base, axis=1, keepdims=True)
    col_first = lax.axis_index("col") * f_local
    offset = seed_ref[0] * jnp.int32(1013904223)
    width = largest_block(f_local, 256)
    for start in range(0, f_local, width):
        columns = lax.broadcasted_iota(jnp.int32, (rows, width), 1) + (col_first + start)
        mixed = (base + columns) * jnp.int32(747796405) + offset
        mixed = mixed ^ (mixed >> 15)
        mixed = mixed * jnp.int32(277803737)
        mixed = mixed ^ (mixed >> 16)
        level = (mixed & 255).astype(jnp.float32)
        grad = grad_ref[:, start : start + width].astype(jnp.float32)
        done = jnp.floor(grad * 4.0 + (level + 0.5) / 256.0) / 4.0
        pieces = [done[i : i + per_col] for i in range(0, rows, per_col)]
        pieces = [p for c in range(CORES) for p in pieces[c::CORES]]
        out_ref[:, start : start + width] = jnp.concatenate(pieces).astype(out_ref.dtype)


def stochastic_round(grad, counter_base, round_seed, per_col):
    vmem = pl.BlockSpec(memory_space=pltpu.VMEM)
    return pl.pallas_call(
        functools.partial(round_kernel, per_col),
        out_shape=jax.ShapeDtypeStruct(grad.shape, jnp.bfloat16),
        in_specs=[pl.BlockSpec(memory_space=pltpu.SMEM), vmem, vmem],
        out_specs=vmem,
        name="quantize",
        cost_estimate=pl.CostEstimate(
            flops=16 * grad.size, bytes_accessed=4 * grad.size, transcendentals=0
        ),
        compiler_params=pltpu.CompilerParams(vmem_limit_bytes=8 * MIB),
    )(round_seed, counter_base[None, :], grad)


def largest_block(length, most):
    return next(b for b in range(min(most, length), 0, -1) if length % b == 0)


def row_start(j, rows, size):
    owner = lax.rem(lax.axis_index("row") - j + rows, rows)
    return pl.multiple_of(owner * size, size)


def project_kernel(n_row, block, *refs):
    q_refs, (w_hbm, keep_ref, give_ref, w_ref, sems) = refs[:n_row], refs[n_row:]
    tr = q_refs[0].shape[0]
    half = tr // CORES
    core = lax.rem(lax.axis_index("col"), CORES)

    def fetch(step):
        ds = pl.ds(pl.multiple_of(step * block, block), block)
        return pltpu.make_async_copy(w_hbm.at[ds, :], w_ref.at[ds, :], sems.at[step])

    steps = w_ref.shape[0] // block
    for step in range(steps):
        fetch(step).start()

    @pl.loop(0, steps)
    def _(step):
        fetch(step).wait()
        ds = pl.ds(pl.multiple_of(step * block, block), block)
        q = jnp.concatenate([q_ref[...] for q_ref in q_refs], axis=0)
        whole = lax.dot_general(
            w_ref[ds, :], q, (((1,), (1,)), ((), ())), preferred_element_type=jnp.float32
        )
        whole = whole.T.astype(jnp.bfloat16)
        for c in range(CORES):

            @pl.when(core == c)
            def _():
                for j in range(n_row):
                    at = pl.ds(row_start(j, n_row, half), half)
                    for k in range(CORES):
                        piece = whole[j * tr + k * half : j * tr + (k + 1) * half]
                        (keep_ref if k == c else give_ref)[at, ds] = piece


def project(q_parts, up_weight):
    n_row = len(q_parts)
    tokens = q_parts[0].shape[0] * n_row
    d_local, f_local = up_weight.shape
    block = largest_block(d_local, 512)
    vmem = pl.BlockSpec(memory_space=pltpu.VMEM)
    return pl.pallas_call(
        functools.partial(project_kernel, n_row, block),
        out_shape=[jax.ShapeDtypeStruct((tokens // CORES, d_local), jnp.bfloat16)] * 2,
        in_specs=[vmem] * n_row + [pl.BlockSpec(memory_space=pl.ANY)],
        out_specs=[vmem] * 2,
        scratch_shapes=[
            pltpu.VMEM(up_weight.shape, up_weight.dtype),
            pltpu.SemaphoreType.DMA((d_local // block,)),
        ],
        name="project",
        cost_estimate=pl.CostEstimate(
            flops=2 * tokens * d_local * f_local,
            bytes_accessed=2 * d_local * f_local,
            transcendentals=0,
        ),
        compiler_params=pltpu.CompilerParams(vmem_limit_bytes=VMEM_PROJECT * MIB),
    )(*q_parts, up_weight)


VMEM_PROJECT = 44
VMEM_WGRAD = 32


def wgrad_kernel(n_row, scaling, *refs):
    q_refs, (mine_ref, other_ref, out_ref, x_ref) = refs[:n_row], refs[n_row:]
    tr = q_refs[0].shape[0]
    half = tr // CORES
    block = out_ref.shape[0]
    core = lax.rem(lax.axis_index("col"), CORES)
    for c in range(CORES):

        @pl.when((pl.program_id(0) == 0) & (core == c))
        def _():
            for j in range(n_row):
                at = pl.ds(row_start(j, n_row, half), half)
                for k in range(CORES):
                    source = mine_ref if k == c else other_ref
                    to = j * tr + k * half
                    x_ref[to : to + half, :] = source[at, :]

    q = jnp.concatenate([q_ref[...] for q_ref in q_refs], axis=0)
    ds = pl.ds(pl.multiple_of(pl.program_id(0) * block, block), block)
    out_ref[...] = scaling * lax.dot_general(
        x_ref[:, ds], q, (((0,), (0,)), ((), ())), preferred_element_type=jnp.float32
    )


def wgrad(q_parts, x_mine, x_other, scaling):
    n_row = len(q_parts)
    tr, f_local = q_parts[0].shape
    tokens, d_local = tr * n_row, x_mine.shape[1]
    block = largest_block(d_local, 512)
    vmem = pl.BlockSpec(memory_space=pltpu.VMEM)
    return pl.pallas_call(
        functools.partial(wgrad_kernel, n_row, scaling),
        grid=(d_local // block,),
        out_shape=jax.ShapeDtypeStruct((d_local, f_local), jnp.float32),
        in_specs=[vmem] * (n_row + 2),
        out_specs=pl.BlockSpec((block, f_local), lambda i: (i, 0)),
        scratch_shapes=[pltpu.VMEM((tokens, d_local), jnp.bfloat16)],
        name="wgrad",
        cost_estimate=pl.CostEstimate(
            flops=2 * tokens * d_local * f_local,
            bytes_accessed=4 * d_local * f_local,
            transcendentals=0,
        ),
        compiler_params=pltpu.CompilerParams(vmem_limit_bytes=VMEM_WGRAD * MIB),
    )(*q_parts, x_mine, x_other)


def shards(activations, up_weight, out_grad, round_seed, counter_base):
    n_row, n_col = lax.axis_size("row"), lax.axis_size("col")
    n_chip = n_col // CORES
    assert n_col % (CORES * n_row) == 0
    per_col, d_local = activations.shape
    tokens = per_col * n_col
    chips = [[chip * CORES + c for chip in range(n_chip)] for c in range(CORES)]
    swap = [(i, i ^ 1) for i in range(n_col)]

    own = stochastic_round(out_grad, counter_base, round_seed, per_col)
    q_parts = [own] + [
        lax.ppermute(own, "row", [(i, (i + j) % n_row) for i in range(n_row)])
        for j in range(1, n_row)
    ]
    copies = jnp.broadcast_to(activations, (n_chip, per_col, d_local))
    x_mine = lax.all_to_all(copies, "col", 0, 0, axis_index_groups=chips)
    x_mine = x_mine.reshape(n_chip * per_col, d_local)
    x_other = lax.ppermute(x_mine, "col", swap)
    keep, give = project(q_parts, up_weight)
    taken = lax.ppermute(give, "col", swap)
    pair = keep.astype(jnp.float32) + taken.astype(jnp.float32)
    pair = pair.astype(jnp.bfloat16).reshape(n_chip, per_col, d_local)
    shares = lax.all_to_all(pair, "col", 0, 0, axis_index_groups=chips)
    weight_grad = wgrad(q_parts, x_mine, x_other, tokens ** (-0.5))
    input_grad = jnp.sum(shares.astype(jnp.float32), axis=0)
    return weight_grad, input_grad.astype(jnp.bfloat16)


def solution(mesh):
    placed = (P("col", "row"), P("row", "col"), P("row", "col"), P(), P("row"))
    return jax.shard_map(
        shards,
        mesh=mesh,
        in_specs=placed,
        out_specs=(P("row", "col"), P("col", "row")),
        check_vma=False,
    )
```

```python
import functools

import jax
import jax.numpy as jnp
from jax import lax
from jax.experimental import pallas as pl
from jax.experimental.pallas import tpu as pltpu
from jax.sharding import PartitionSpec as P


CORES = 2
LANES = 256
MIB = 2**20


def round_kernel(per_col, cuts, seed_ref, base_hbm, grad_hbm, x_hbm, *refs):
    n_cut = len(cuts) - 1
    out_refs, refs = refs[:n_cut], refs[n_cut:]
    copies_hbm, base_ref, grad_ref, x_ref, sems, copy_sems = refs
    loads = [
        pltpu.make_async_copy(base_hbm, base_ref, sems.at[0]),
        pltpu.make_async_copy(x_hbm, x_ref, sems.at[1]),
        pltpu.make_async_copy(grad_hbm, grad_ref, sems.at[2]),
    ]
    for load in loads:
        load.start()
    stores = [
        pltpu.make_async_copy(x_ref, copies_hbm.at[i], copy_sems.at[i])
        for i in range(copies_hbm.shape[0])
    ]
    loads[0].wait()
    rows, f_local = grad_ref.shape
    shape = (rows, rows)
    diagonal = lax.broadcasted_iota(jnp.int32, shape, 0) == lax.broadcasted_iota(
        jnp.int32, shape, 1
    )
    base = jnp.where(diagonal, jnp.broadcast_to(base_ref[...], shape), 0)
    base = jnp.sum(base, axis=1, keepdims=True)
    col_first = lax.axis_index("col") * f_local
    offset = seed_ref[0] * jnp.int32(1013904223)
    loads[1].wait()
    for store in stores:
        store.start()
    loads[2].wait()
    for out_ref, cut, end in zip(out_refs, cuts, cuts[1:], strict=False):
        width = largest_block(end - cut, 256)
        for start in range(cut, end, width):
            columns = lax.broadcasted_iota(jnp.int32, (rows, width), 1)
            counter = base + (columns + (col_first + start))
            mixed = counter * jnp.int32(747796405) + offset
            mixed = mixed ^ (mixed >> 15)
            mixed = mixed * jnp.int32(277803737)
            mixed = mixed ^ (mixed >> 16)
            level = (mixed & 255).astype(jnp.float32)
            grad = grad_ref[:, start : start + width].astype(jnp.float32)
            done = jnp.floor(grad * 4.0 + (level + 0.5) / 256.0) / 4.0
            pieces = [done[i : i + per_col] for i in range(0, rows, per_col)]
            pieces = [p for c in range(CORES) for p in pieces[c::CORES]]
            at = slice(start - cut, start - cut + width)
            out_ref[:, at] = jnp.concatenate(pieces).astype(out_ref.dtype)
    for store in stores:
        store.wait()


def stochastic_round(grad, counter_base, round_seed, activations, cuts, n_chip):
    per_col, d_local = activations.shape
    rows = grad.shape[0]
    vmem = pl.BlockSpec(memory_space=pltpu.VMEM)
    hbm = pl.BlockSpec(memory_space=pltpu.HBM)
    *parts, copies = pl.pallas_call(
        functools.partial(round_kernel, per_col, cuts),
        out_shape=[
            jax.ShapeDtypeStruct((rows, end - cut), jnp.bfloat16)
            for cut, end in zip(cuts, cuts[1:], strict=False)
        ]
        + [jax.ShapeDtypeStruct((n_chip, per_col, d_local), activations.dtype)],
        in_specs=[pl.BlockSpec(memory_space=pltpu.SMEM)] + [hbm] * 3,
        out_specs=[vmem] * (len(cuts) - 1) + [hbm],
        scratch_shapes=[
            pltpu.VMEM((1, rows), jnp.int32),
            pltpu.VMEM(grad.shape, grad.dtype),
            pltpu.VMEM(activations.shape, activations.dtype),
            pltpu.SemaphoreType.DMA((3,)),
            pltpu.SemaphoreType.DMA((n_chip,)),
        ],
        name="quantize",
        cost_estimate=pl.CostEstimate(
            flops=16 * grad.size, bytes_accessed=4 * grad.size, transcendentals=0
        ),
        compiler_params=pltpu.CompilerParams(vmem_limit_bytes=8 * MIB),
    )(round_seed, *in_hbm(counter_base[None, :], grad, activations))
    return parts, copies


def in_hbm(*arrays):
    return [pltpu.with_memory_space_constraint(a, pltpu.HBM) for a in arrays]


def largest_block(length, most):
    return next(b for b in range(min(most, length), 0, -1) if length % b == 0)


def row_start(j, rows, size):
    owner = lax.rem(lax.axis_index("row") - j + rows, rows)
    return pl.multiple_of(owner * size, size)


def project_kernel(n_row, first, final, f_from, block, *refs):
    q_refs, refs = refs[:n_row], refs[n_row:]
    acc_ref = None
    if not first:
        acc_ref, refs = refs[0], refs[1:]
    w_hbm, *outs, w_ref, sems = refs
    tr, f_len = q_refs[0].shape
    half = tr // CORES
    core = lax.rem(lax.axis_index("col"), CORES)

    def fetch(step):
        ds = pl.ds(pl.multiple_of(step * block, block), block)
        return pltpu.make_async_copy(
            w_hbm.at[ds, pl.ds(f_from, f_len)], w_ref.at[ds, :], sems.at[step]
        )

    steps = w_ref.shape[0] // block
    for step in range(steps):
        fetch(step).start()

    @pl.loop(0, steps)
    def _(step):
        fetch(step).wait()
        ds = pl.ds(pl.multiple_of(step * block, block), block)
        q = jnp.concatenate([q_ref[...] for q_ref in q_refs], axis=0)
        part = lax.dot_general(
            w_ref[ds, :], q, (((1,), (1,)), ((), ())), preferred_element_type=jnp.float32
        )
        if acc_ref is not None:
            part = part + acc_ref[ds, :]
        if not final:
            outs[0][ds, :] = part
            return
        whole = part.T.astype(jnp.bfloat16)
        for c in range(CORES):

            @pl.when(core == c)
            def _():
                for j in range(n_row):
                    at = pl.ds(row_start(j, n_row, half), half)
                    for k in range(CORES):
                        piece = whole[j * tr + k * half : j * tr + (k + 1) * half]
                        outs[0 if k == c else 1][at, ds] = piece


def project(q_parts, up_weight, acc, f_from, final):
    n_row = len(q_parts)
    tr, f_len = q_parts[0].shape
    tokens = tr * n_row
    d_local = up_weight.shape[0]
    block = largest_block(d_local, 512)
    vmem = pl.BlockSpec(memory_space=pltpu.VMEM)
    if final:
        out = [jax.ShapeDtypeStruct((tokens // CORES, d_local), jnp.bfloat16)] * 2
    else:
        out = [jax.ShapeDtypeStruct((d_local, tokens), jnp.float32)]
    held = [] if acc is None else [acc]
    return pl.pallas_call(
        functools.partial(project_kernel, n_row, acc is None, final, f_from, block),
        out_shape=out,
        in_specs=[vmem] * (n_row + len(held)) + [pl.BlockSpec(memory_space=pltpu.HBM)],
        out_specs=[vmem] * len(out),
        scratch_shapes=[
            pltpu.VMEM((d_local, f_len), up_weight.dtype),
            pltpu.SemaphoreType.DMA((d_local // block,)),
        ],
        name="project",
        cost_estimate=pl.CostEstimate(
            flops=2 * tokens * d_local * f_len,
            bytes_accessed=2 * d_local * f_len,
            transcendentals=0,
        ),
        compiler_params=pltpu.CompilerParams(vmem_limit_bytes=VMEM_PROJECT * MIB),
    )(*q_parts, *held, *in_hbm(up_weight))


VMEM_PROJECT = 24
VMEM_WGRAD = 32


def wgrad_kernel(n_row, n_cut, scaling, *refs):
    q_refs, refs = refs[: n_row * n_cut], refs[n_row * n_cut :]
    mine_ref, other_ref, out_hbm, x_ref, q_ref, held, sems = refs
    tr = q_refs[0].shape[0]
    half = tr // CORES
    slots, block, _ = held.shape
    core = lax.rem(lax.axis_index("col"), CORES)
    for c in range(CORES):

        @pl.when(core == c)
        def _():
            for j in range(n_row):
                at = pl.ds(row_start(j, n_row, half), half)
                for k in range(CORES):
                    source = mine_ref if k == c else other_ref
                    to = j * tr + k * half
                    x_ref[to : to + half, :] = source[at, :]

    for j in range(n_row):
        start = 0
        for i in range(n_cut):
            part = q_refs[i * n_row + j]
            end = start + part.shape[1]
            q_ref[j * tr : (j + 1) * tr, start:end] = part[...]
            start = end

    def store(step):
        slot = lax.rem(step, slots)
        ds = pl.ds(pl.multiple_of(step * block, block), block)
        return pltpu.make_async_copy(held.at[slot], out_hbm.at[ds, :], sems.at[slot])

    steps = out_hbm.shape[0] // block

    @pl.loop(0, steps)
    def _(step):
        @pl.when(step >= slots)
        def _():
            store(step - slots).wait()

        ds = pl.ds(pl.multiple_of(step * block, block), block)
        held[lax.rem(step, slots)] = scaling * lax.dot_general(
            x_ref[:, ds],
            q_ref[...],
            (((0,), (0,)), ((), ())),
            preferred_element_type=jnp.float32,
        )
        store(step).start()

    for step in range(max(steps - slots, 0), steps):
        store(step).wait()


def wgrad(q_cuts, x_mine, x_other, scaling):
    n_cut, n_row = len(q_cuts), len(q_cuts[0])
    tr = q_cuts[0][0].shape[0]
    f_local = sum(parts[0].shape[1] for parts in q_cuts)
    tokens, d_local = tr * n_row, x_mine.shape[1]
    block = largest_block(d_local, 256)
    slots = min(3, d_local // block)
    vmem = pl.BlockSpec(memory_space=pltpu.VMEM)
    return pl.pallas_call(
        functools.partial(wgrad_kernel, n_row, n_cut, scaling),
        out_shape=jax.ShapeDtypeStruct((d_local, f_local), jnp.float32),
        in_specs=[vmem] * (n_row * n_cut + 2),
        out_specs=pl.BlockSpec(memory_space=pltpu.HBM),
        scratch_shapes=[
            pltpu.VMEM((tokens, d_local), jnp.bfloat16),
            pltpu.VMEM((tokens, f_local), jnp.bfloat16),
            pltpu.VMEM((slots, block, f_local), jnp.float32),
            pltpu.SemaphoreType.DMA((slots,)),
        ],
        name="wgrad",
        cost_estimate=pl.CostEstimate(
            flops=2 * tokens * d_local * f_local,
            bytes_accessed=4 * d_local * f_local,
            transcendentals=0,
        ),
        compiler_params=pltpu.CompilerParams(vmem_limit_bytes=VMEM_WGRAD * MIB),
    )(*[part for parts in q_cuts for part in parts], x_mine, x_other)


def shards(activations, up_weight, out_grad, round_seed, counter_base):
    n_row, n_col = lax.axis_size("row"), lax.axis_size("col")
    n_chip = n_col // CORES
    assert n_col % (CORES * n_row) == 0
    per_col, d_local = activations.shape
    tokens = per_col * n_col
    chips = [[chip * CORES + c for chip in range(n_chip)] for c in range(CORES)]
    swap = [(i, i ^ 1) for i in range(n_col)]

    f_local = out_grad.shape[1]
    middle = f_local // (2 * LANES) * LANES
    cuts = (0, middle, f_local)
    shifts = [[(i, (i + j) % n_row) for i in range(n_row)] for j in range(1, n_row)]
    owns, copies = stochastic_round(
        out_grad, counter_base, round_seed, activations, cuts, n_chip
    )
    q_a = [owns[0]] + [lax.ppermute(owns[0], "row", shift) for shift in shifts]
    q_b = [owns[1]] + [lax.ppermute(owns[1], "row", shift) for shift in shifts]
    x_mine = lax.all_to_all(copies, "col", 0, 0, axis_index_groups=chips)
    x_mine = x_mine.reshape(n_chip * per_col, d_local)
    x_other = lax.ppermute(x_mine, "col", swap)
    (acc,) = project(q_a, up_weight, None, 0, False)
    keep, give = project(q_b, up_weight, acc, middle, True)
    taken = lax.ppermute(give, "col", swap)
    pair = keep.astype(jnp.float32) + taken.astype(jnp.float32)
    pair = pair.astype(jnp.bfloat16).reshape(n_chip, per_col, d_local)
    shares = lax.all_to_all(pair, "col", 0, 0, axis_index_groups=chips)
    weight_grad = wgrad((q_a, q_b), x_mine, x_other, tokens ** (-0.5))
    input_grad = jnp.sum(shares.astype(jnp.float32), axis=0)
    return weight_grad, input_grad.astype(jnp.bfloat16)


def solution(mesh):
    placed = (P("col", "row"), P("row", "col"), P("row", "col"), P(), P("row"))
    return jax.shard_map(
        shards,
        mesh=mesh,
        in_specs=placed,
        out_specs=(P("row", "col"), P("col", "row")),
        check_vma=False,
    )
```

```python
import functools

import jax
import jax.numpy as jnp
from jax import lax
from jax.experimental import pallas as pl
from jax.experimental.pallas import tpu as pltpu
from jax.sharding import PartitionSpec as P


CORES = 2
LANES = 256
MIB = 2**20


def round_kernel(per_col, cuts, seed_ref, base_hbm, grad_hbm, x_hbm, w_hbm, *refs):
    n_cut = len(cuts) - 1
    out_refs, refs = refs[:n_cut], refs[n_cut:]
    copies_hbm, head_ref, base_ref, grad_ref, x_ref, sems, copy_sems = refs
    loads = [
        pltpu.make_async_copy(x_hbm, x_ref, sems.at[0]),
        pltpu.make_async_copy(base_hbm, base_ref, sems.at[1]),
    ] + [
        pltpu.make_async_copy(
            grad_hbm.at[:, cut:end], grad_ref.at[:, cut:end], sems.at[2 + i]
        )
        for i, (cut, end) in enumerate(zip(cuts, cuts[1:], strict=False))
    ]
    loads.append(
        pltpu.make_async_copy(
            w_hbm.at[: head_ref.shape[0], : head_ref.shape[1]], head_ref, sems.at[1 + len(cuts)]
        )
    )
    for load in loads:
        load.start()
    stores = [
        pltpu.make_async_copy(x_ref, copies_hbm.at[i], copy_sems.at[i])
        for i in range(copies_hbm.shape[0])
    ]
    loads[1].wait()
    rows, f_local = grad_ref.shape
    shape = (rows, rows)
    diagonal = lax.broadcasted_iota(jnp.int32, shape, 0) == lax.broadcasted_iota(
        jnp.int32, shape, 1
    )
    base = jnp.where(diagonal, jnp.broadcast_to(base_ref[...], shape), 0)
    base = jnp.sum(base, axis=1, keepdims=True)
    col_first = lax.axis_index("col") * f_local
    offset = seed_ref[0] * jnp.int32(1013904223)
    loads[0].wait()
    for store in stores:
        store.start()
    for out_ref, load, cut, end in zip(out_refs, loads[2:-1], cuts, cuts[1:], strict=False):
        load.wait()
        width = largest_block(end - cut, 256)
        for start in range(cut, end, width):
            columns = lax.broadcasted_iota(jnp.int32, (rows, width), 1)
            counter = base + (columns + (col_first + start))
            mixed = counter * jnp.int32(747796405) + offset
            mixed = mixed ^ (mixed >> 15)
            mixed = mixed * jnp.int32(277803737)
            mixed = mixed ^ (mixed >> 16)
            level = (mixed & 255).astype(jnp.float32)
            grad = grad_ref[:, start : start + width].astype(jnp.float32)
            done = jnp.floor(grad * 4.0 + (level + 0.5) / 256.0) / 4.0
            pieces = [done[i : i + per_col] for i in range(0, rows, per_col)]
            pieces = [p for c in range(CORES) for p in pieces[c::CORES]]
            at = slice(start - cut, start - cut + width)
            out_ref[:, at] = jnp.concatenate(pieces).astype(out_ref.dtype)
    for store in stores:
        store.wait()
    loads[-1].wait()


def stochastic_round(
    grad, counter_base, round_seed, activations, up_weight, cuts, n_chip
):
    per_col, d_local = activations.shape
    rows = grad.shape[0]
    vmem = pl.BlockSpec(memory_space=pltpu.VMEM)
    hbm = pl.BlockSpec(memory_space=pltpu.HBM)
    *parts, copies, head = pl.pallas_call(
        functools.partial(round_kernel, per_col, cuts),
        out_shape=[
            jax.ShapeDtypeStruct((rows, end - cut), jnp.bfloat16)
            for cut, end in zip(cuts, cuts[1:], strict=False)
        ]
        + [
            jax.ShapeDtypeStruct((n_chip, per_col, d_local), activations.dtype),
            jax.ShapeDtypeStruct((project_block(d_local), cuts[1]), up_weight.dtype),
        ],
        in_specs=[pl.BlockSpec(memory_space=pltpu.SMEM)] + [hbm] * 4,
        out_specs=[vmem] * (len(cuts) - 1) + [hbm, vmem],
        scratch_shapes=[
            pltpu.VMEM((1, rows), jnp.int32),
            pltpu.VMEM(grad.shape, grad.dtype),
            pltpu.VMEM(activations.shape, activations.dtype),
            pltpu.SemaphoreType.DMA((2 + len(cuts),)),
            pltpu.SemaphoreType.DMA((n_chip,)),
        ],
        name="quantize",
        cost_estimate=pl.CostEstimate(
            flops=16 * grad.size, bytes_accessed=4 * grad.size, transcendentals=0
        ),
        compiler_params=pltpu.CompilerParams(vmem_limit_bytes=8 * MIB),
    )(round_seed, *in_hbm(counter_base[None, :], grad, activations, up_weight))
    return parts, copies, head


def in_hbm(*arrays):
    return [pltpu.with_memory_space_constraint(a, pltpu.HBM) for a in arrays]


def largest_block(length, most):
    return next(b for b in range(min(most, length), 0, -1) if length % b == 0)


def row_start(j, rows, size):
    owner = lax.rem(lax.axis_index("row") - j + rows, rows)
    return pl.multiple_of(owner * size, size)


def project_block(d_local):
    return largest_block(d_local, 512)


def project_kernel(n_row, final, f_from, block, *refs):
    q_refs, refs = refs[:n_row], refs[n_row:]
    if final:
        acc_ref, head_ref, w_hbm, keep_ref, give_ref, w_ref, sems, turned_ref = refs
    else:
        head_ref, w_hbm, acc_ref, ahead_ref, w_ref, sems, ahead_sem = refs
    head = head_ref.shape[0] // block
    tr, f_len = q_refs[0].shape
    half = tr // CORES
    core = lax.rem(lax.axis_index("col"), CORES)
    steps = w_ref.shape[0] // block

    def rows_of(step):
        return pl.ds(pl.multiple_of(step * block, block), block)

    def fetch(step):
        source = w_hbm.at[rows_of(step), pl.ds(f_from, f_len)]
        return pltpu.make_async_copy(source, w_ref.at[rows_of(step), :], sems.at[step])

    def multiply(step, weight_ref):
        at_d = rows_of(step)
        part = lax.dot_general(
            weight_ref[at_d, :],
            jnp.concatenate([q_ref[...] for q_ref in q_refs], axis=0),
            (((1,), (1,)), ((), ())),
            preferred_element_type=jnp.float32,
        )
        if not final:
            acc_ref[at_d, :] = part
            return
        turned_ref[...] = (part + acc_ref[at_d, :]).astype(jnp.bfloat16).T
        for j in range(n_row):
            at = pl.ds(row_start(j, n_row, half), half)
            for out_ref, c in ((keep_ref, core), (give_ref, 1 - core)):
                source = pl.multiple_of(j * tr + c * half, half)
                out_ref[at, at_d] = turned_ref[pl.ds(source, half), :]

    for step in range(head, steps):
        fetch(step).start()
    if not final:
        f_next = f_from + f_len
        source = w_hbm.at[: ahead_ref.shape[0], f_next : f_next + ahead_ref.shape[1]]
        ahead = pltpu.make_async_copy(source, ahead_ref, ahead_sem)
        ahead.start()

    @pl.loop(0, head)
    def _(step):
        multiply(step, head_ref)

    @pl.loop(head, steps)
    def _(step):
        fetch(step).wait()
        multiply(step, w_ref)

    if not final:
        ahead.wait()


def project(q_parts, up_weight, f_from, held):
    n_row = len(q_parts)
    tr, f_len = q_parts[0].shape
    tokens = tr * n_row
    d_local, f_local = up_weight.shape
    final = len(held) > 1
    block = project_block(d_local)
    steps = d_local // block
    vmem = pl.BlockSpec(memory_space=pltpu.VMEM)
    scratch = [
        pltpu.VMEM((d_local, f_len), up_weight.dtype),
        pltpu.SemaphoreType.DMA((steps,)),
    ]
    if final:
        scratch.append(pltpu.VMEM((tokens, block), jnp.bfloat16))
        out = [jax.ShapeDtypeStruct((tokens // CORES, d_local), jnp.bfloat16)] * 2
    else:
        ahead = (block * max(1, steps // 4), f_local - f_len)
        out = [
            jax.ShapeDtypeStruct((d_local, tokens), jnp.float32),
            jax.ShapeDtypeStruct(ahead, up_weight.dtype),
        ]
        scratch.append(pltpu.SemaphoreType.DMA(()))
    return pl.pallas_call(
        functools.partial(project_kernel, n_row, final, f_from, block),
        out_shape=out,
        in_specs=[vmem] * (n_row + len(held)) + [pl.BlockSpec(memory_space=pltpu.HBM)],
        out_specs=[vmem] * 2,
        scratch_shapes=scratch,
        name="project",
        cost_estimate=pl.CostEstimate(
            flops=2 * tokens * d_local * f_len,
            bytes_accessed=2 * d_local * f_len,
            transcendentals=0,
        ),
        compiler_params=pltpu.CompilerParams(vmem_limit_bytes=VMEM_PROJECT * MIB),
    )(*q_parts, *held, *in_hbm(up_weight))


VMEM_PROJECT = 28
VMEM_WGRAD = 32


def pair_kernel(keep_ref, taken_ref, out_ref):
    total = keep_ref[...].astype(jnp.float32) + taken_ref[...].astype(jnp.float32)
    out_ref[...] = total.astype(out_ref.dtype)


def pair_sum(keep, taken):
    vmem = pl.BlockSpec(memory_space=pltpu.VMEM)
    return pl.pallas_call(
        pair_kernel,
        out_shape=jax.ShapeDtypeStruct(keep.shape, keep.dtype),
        in_specs=[vmem] * 2,
        out_specs=vmem,
        name="pairsum",
        cost_estimate=pl.CostEstimate(
            flops=keep.size, bytes_accessed=6 * keep.size, transcendentals=0
        ),
        compiler_params=pltpu.CompilerParams(vmem_limit_bytes=8 * MIB),
    )(keep, taken)


def wgrad_kernel(n_row, n_cut, scaling, *refs):
    q_refs, refs = refs[: n_row * n_cut], refs[n_row * n_cut :]
    mine_ref, other_ref, out_hbm, x_ref, q_ref, held, sems = refs
    tr = q_refs[0].shape[0]
    half = tr // CORES
    slots, block, _ = held.shape
    core = lax.rem(lax.axis_index("col"), CORES)
    for c in range(CORES):

        @pl.when(core == c)
        def _():
            for j in range(n_row):
                at = pl.ds(row_start(j, n_row, half), half)
                for k in range(CORES):
                    source = mine_ref if k == c else other_ref
                    to = j * tr + k * half
                    x_ref[to : to + half, :] = source[at, :]

    for j in range(n_row):
        start = 0
        for i in range(n_cut):
            part = q_refs[i * n_row + j]
            end = start + part.shape[1]
            q_ref[j * tr : (j + 1) * tr, start:end] = part[...]
            start = end

    f_local = out_hbm.shape[1]
    cuts = (0, f_local // (2 * LANES) * LANES, f_local)
    sides = [slice(*side) for side in zip(cuts, cuts[1:], strict=False)]

    def store(step, side):
        slot = lax.rem(step, slots)
        rows = pl.ds(pl.multiple_of(step * block, block), block)
        return pltpu.make_async_copy(
            held.at[slot, :, sides[side]], out_hbm.at[rows, sides[side]], sems.at[slot, side]
        )

    steps = out_hbm.shape[0] // block

    @pl.loop(0, steps)
    def _(step):
        rows = pl.ds(pl.multiple_of(step * block, block), block)
        for side in range(len(sides)):

            @pl.when(step >= slots)
            def _():
                store(step - slots, side).wait()

            held[lax.rem(step, slots), :, sides[side]] = scaling * lax.dot_general(
                x_ref[:, rows],
                q_ref[:, sides[side]],
                (((0,), (0,)), ((), ())),
                preferred_element_type=jnp.float32,
            )
            store(step, side).start()

    for step in range(max(steps - slots, 0), steps):
        for side in range(len(sides)):
            store(step, side).wait()


def wgrad(q_cuts, x_mine, x_other, scaling):
    n_cut, n_row = len(q_cuts), len(q_cuts[0])
    tr = q_cuts[0][0].shape[0]
    f_local = sum(parts[0].shape[1] for parts in q_cuts)
    tokens, d_local = tr * n_row, x_mine.shape[1]
    block = largest_block(d_local, 256)
    slots = min(3, d_local // block)
    vmem = pl.BlockSpec(memory_space=pltpu.VMEM)
    return pl.pallas_call(
        functools.partial(wgrad_kernel, n_row, n_cut, scaling),
        out_shape=jax.ShapeDtypeStruct((d_local, f_local), jnp.float32),
        in_specs=[vmem] * (n_row * n_cut + 2),
        out_specs=pl.BlockSpec(memory_space=pltpu.HBM),
        scratch_shapes=[
            pltpu.VMEM((tokens, d_local), jnp.bfloat16),
            pltpu.VMEM((tokens, f_local), jnp.bfloat16),
            pltpu.VMEM((slots, block, f_local), jnp.float32),
            pltpu.SemaphoreType.DMA((slots, 2)),
        ],
        name="wgrad",
        cost_estimate=pl.CostEstimate(
            flops=2 * tokens * d_local * f_local,
            bytes_accessed=4 * d_local * f_local,
            transcendentals=0,
        ),
        compiler_params=pltpu.CompilerParams(vmem_limit_bytes=VMEM_WGRAD * MIB),
    )(*[part for parts in q_cuts for part in parts], x_mine, x_other)


def shards(activations, up_weight, out_grad, round_seed, counter_base):
    n_row, n_col = lax.axis_size("row"), lax.axis_size("col")
    n_chip = n_col // CORES
    assert n_col % (CORES * n_row) == 0
    per_col, d_local = activations.shape
    tokens = per_col * n_col
    chips = [[chip * CORES + c for chip in range(n_chip)] for c in range(CORES)]
    swap = [(i, i ^ 1) for i in range(n_col)]

    f_local = out_grad.shape[1]
    middle = f_local // (2 * LANES) * LANES
    cuts = (0, middle, f_local)
    shifts = [[(i, (i + j) % n_row) for i in range(n_row)] for j in range(1, n_row)]
    owns, copies, head = stochastic_round(
        out_grad, counter_base, round_seed, activations, up_weight, cuts, n_chip
    )
    q_a = [owns[0]] + [lax.ppermute(owns[0], "row", shift) for shift in shifts]
    q_b = [owns[1]] + [lax.ppermute(owns[1], "row", shift) for shift in shifts]
    x_mine = lax.all_to_all(copies, "col", 0, 0, axis_index_groups=chips)
    x_mine = x_mine.reshape(n_chip * per_col, d_local)
    x_other = lax.ppermute(x_mine, "col", swap)
    held = project(q_a, up_weight, 0, (head,))
    keep, give = project(q_b, up_weight, middle, held)
    taken = lax.ppermute(give, "col", swap)
    pair = pair_sum(keep, taken).reshape(n_chip, per_col, d_local)
    shares = lax.all_to_all(pair, "col", 0, 0, axis_index_groups=chips)
    weight_grad = wgrad((q_a, q_b), x_mine, x_other, tokens ** (-0.5))
    input_grad = jnp.sum(shares.astype(jnp.float32), axis=0)
    return weight_grad, input_grad.astype(jnp.bfloat16)


def solution(mesh):
    placed = (P("col", "row"), P("row", "col"), P("row", "col"), P(), P("row"))
    return jax.shard_map(
        shards,
        mesh=mesh,
        in_specs=placed,
        out_specs=(P("row", "col"), P("col", "row")),
        check_vma=False,
    )
```

```python
import functools

import jax
import jax.numpy as jnp
from jax import lax
from jax.experimental import pallas as pl
from jax.experimental.pallas import tpu as pltpu
from jax.sharding import PartitionSpec as P


CORES = 2
LANES = 256
MIB = 2**20


def round_kernel(per_col, cuts, seed_ref, base_hbm, grad_hbm, x_hbm, w_hbm, *refs):
    n_cut = len(cuts) - 1
    out_refs, refs = refs[:n_cut], refs[n_cut:]
    copies_hbm, head_ref, base_ref, grad_ref, x_ref, sems, copy_sems = refs
    loads = [
        pltpu.make_async_copy(x_hbm, x_ref, sems.at[0]),
        pltpu.make_async_copy(base_hbm, base_ref, sems.at[1]),
    ] + [
        pltpu.make_async_copy(
            grad_hbm.at[:, cut:end], grad_ref.at[:, cut:end], sems.at[2 + i]
        )
        for i, (cut, end) in enumerate(zip(cuts, cuts[1:], strict=False))
    ]
    loads.append(
        pltpu.make_async_copy(
            w_hbm.at[: head_ref.shape[0], : head_ref.shape[1]], head_ref, sems.at[1 + len(cuts)]
        )
    )
    for load in loads:
        load.start()
    stores = [
        pltpu.make_async_copy(x_ref, copies_hbm.at[i], copy_sems.at[i])
        for i in range(copies_hbm.shape[0])
    ]
    loads[1].wait()
    rows, f_local = grad_ref.shape
    shape = (rows, rows)
    diagonal = lax.broadcasted_iota(jnp.int32, shape, 0) == lax.broadcasted_iota(
        jnp.int32, shape, 1
    )
    base = jnp.where(diagonal, jnp.broadcast_to(base_ref[...], shape), 0)
    base = jnp.sum(base, axis=1, keepdims=True)
    col_first = lax.axis_index("col") * f_local
    offset = seed_ref[0] * jnp.int32(1013904223)
    loads[0].wait()
    for store in stores:
        store.start()
    for out_ref, load, cut, end in zip(out_refs, loads[2:-1], cuts, cuts[1:], strict=False):
        load.wait()
        width = largest_block(end - cut, 256)
        for start in range(cut, end, width):
            columns = lax.broadcasted_iota(jnp.int32, (rows, width), 1)
            counter = base + (columns + (col_first + start))
            mixed = counter * jnp.int32(747796405) + offset
            mixed = mixed ^ (mixed >> 15)
            mixed = mixed * jnp.int32(277803737)
            mixed = mixed ^ (mixed >> 16)
            level = (mixed & 255).astype(jnp.float32)
            grad = grad_ref[:, start : start + width].astype(jnp.float32)
            done = jnp.floor(grad * 4.0 + (level + 0.5) / 256.0) / 4.0
            pieces = [done[i : i + per_col] for i in range(0, rows, per_col)]
            pieces = [p for c in range(CORES) for p in pieces[c::CORES]]
            at = slice(start - cut, start - cut + width)
            out_ref[:, at] = jnp.concatenate(pieces).astype(out_ref.dtype)
    for store in stores:
        store.wait()
    loads[-1].wait()


def stochastic_round(
    grad, counter_base, round_seed, activations, up_weight, cuts, n_chip
):
    per_col, d_local = activations.shape
    rows = grad.shape[0]
    vmem = pl.BlockSpec(memory_space=pltpu.VMEM)
    hbm = pl.BlockSpec(memory_space=pltpu.HBM)
    *parts, copies, head = pl.pallas_call(
        functools.partial(round_kernel, per_col, cuts),
        out_shape=[
            jax.ShapeDtypeStruct((rows, end - cut), jnp.bfloat16)
            for cut, end in zip(cuts, cuts[1:], strict=False)
        ]
        + [
            pltpu.HBM((n_chip, per_col, d_local), activations.dtype),
            jax.ShapeDtypeStruct((project_block(d_local), cuts[1]), up_weight.dtype),
        ],
        in_specs=[pl.BlockSpec(memory_space=pltpu.SMEM)] + [hbm] * 4,
        out_specs=[vmem] * (len(cuts) - 1) + [hbm, vmem],
        scratch_shapes=[
            pltpu.VMEM((1, rows), jnp.int32),
            pltpu.VMEM(grad.shape, grad.dtype),
            pltpu.VMEM(activations.shape, activations.dtype),
            pltpu.SemaphoreType.DMA((2 + len(cuts),)),
            pltpu.SemaphoreType.DMA((n_chip,)),
        ],
        name="quantize",
        cost_estimate=pl.CostEstimate(
            flops=16 * grad.size, bytes_accessed=4 * grad.size, transcendentals=0
        ),
        compiler_params=pltpu.CompilerParams(vmem_limit_bytes=8 * MIB),
    )(round_seed, *in_hbm(counter_base[None, :], grad, activations, up_weight))
    return parts, copies, head


def in_hbm(*arrays):
    return [pltpu.with_memory_space_constraint(a, pltpu.HBM) for a in arrays]


def largest_block(length, most):
    return next(b for b in range(min(most, length), 0, -1) if length % b == 0)


def row_start(j, rows, size):
    owner = lax.rem(lax.axis_index("row") - j + rows, rows)
    return pl.multiple_of(owner * size, size)


def project_block(d_local):
    return largest_block(d_local, 512)


def project_kernel(n_row, first, final, d_from, f_from, next_at, block, *refs):
    q_refs, refs = refs[:n_row], list(refs[n_row:])
    sum_ref = None if first else refs.pop(0)
    head_ref, w_hbm = refs.pop(0), refs.pop(0)
    out_refs = [refs.pop(0) for _ in range(CORES if final else 1)]
    ahead_ref = None if next_at is None else refs.pop(0)
    w_ref, sems = refs.pop(0), refs.pop(0)
    head = head_ref.shape[0] // block
    tr, f_len = q_refs[0].shape
    half = tr // CORES
    core = lax.rem(lax.axis_index("col"), CORES)
    steps = out_refs[0].shape[1 if final else 0] // block

    def rows_of(step, start=0):
        return pl.ds(pl.multiple_of(step * block + start, block), block)

    def fetch(step):
        source = w_hbm.at[rows_of(step, d_from), pl.ds(f_from, f_len)]
        return pltpu.make_async_copy(source, w_ref.at[rows_of(step - head), :], sems.at[step])

    def multiply(step, weight_ref, weight_step):
        at_d = rows_of(step)
        part = lax.dot_general(
            weight_ref[rows_of(weight_step), :],
            jnp.concatenate([q_ref[...] for q_ref in q_refs], axis=0),
            (((1,), (1,)), ((), ())),
            preferred_element_type=jnp.float32,
        )
        if sum_ref is not None:
            part = part + sum_ref[rows_of(step, d_from), :]
        if not final:
            out_refs[0][at_d, :] = part
            return
        turned_ref = refs[0]
        turned_ref[...] = part.astype(jnp.bfloat16).T
        for j in range(n_row):
            at = pl.ds(row_start(j, n_row, half), half)
            for out_ref, c in zip(out_refs, (core, 1 - core), strict=True):
                source = pl.multiple_of(j * tr + c * half, half)
                out_ref[at, at_d] = turned_ref[pl.ds(source, half), :]

    for step in range(head, steps):
        fetch(step).start()
    if ahead_ref is not None:
        d_next, f_next = next_at
        n_d, n_f = ahead_ref.shape
        source = w_hbm.at[d_next : d_next + n_d, f_next : f_next + n_f]
        ahead = pltpu.make_async_copy(source, ahead_ref, sems.at[steps])
        ahead.start()

    @pl.loop(0, head)
    def _(step):
        multiply(step, head_ref, step)

    if head < steps:

        @pl.loop(head, steps)
        def _(step):
            fetch(step).wait()
            multiply(step, w_ref, step - head)

    if ahead_ref is not None:
        ahead.wait()


def project(q_parts, up_weight, total, head, d_cut, f_from, final, following=None):
    n_row = len(q_parts)
    tr, f_len = q_parts[0].shape
    tokens = tr * n_row
    d_from, d_to = d_cut
    size = d_to - d_from
    block = project_block(up_weight.shape[0])
    steps = size // block
    vmem = pl.BlockSpec(memory_space=pltpu.VMEM)
    scratch = [
        pltpu.VMEM((max(size - head.shape[0], block), f_len), up_weight.dtype),
        pltpu.SemaphoreType.DMA((steps + 1,)),
    ]
    if final:
        scratch.append(pltpu.VMEM((tokens, block), jnp.bfloat16))
        out = [jax.ShapeDtypeStruct((tokens // CORES, size), jnp.bfloat16)] * CORES
    else:
        out = [jax.ShapeDtypeStruct((size, tokens), jnp.float32)]
    next_at = None
    if following is not None:
        next_at = tuple(start for start, _ in following)
        shape = tuple(end - start for start, end in following)
        out.append(jax.ShapeDtypeStruct(shape, up_weight.dtype))
    before = [] if total is None else [total]
    return pl.pallas_call(
        functools.partial(
            project_kernel, n_row, total is None, final, d_from, f_from, next_at, block
        ),
        out_shape=out,
        in_specs=[vmem] * (n_row + len(before) + 1) + [pl.BlockSpec(memory_space=pltpu.HBM)],
        out_specs=[vmem] * len(out),
        scratch_shapes=scratch,
        name="project",
        cost_estimate=pl.CostEstimate(
            flops=2 * tokens * size * f_len,
            bytes_accessed=2 * size * f_len,
            transcendentals=0,
        ),
        compiler_params=pltpu.CompilerParams(vmem_limit_bytes=VMEM_PROJECT * MIB),
    )(*q_parts, *before, head, *in_hbm(up_weight))


VMEM_PROJECT = 28
VMEM_WGRAD = 32


def pair_kernel(at, keep_ref, taken_ref, *refs):
    out_hbm, sum_ref, sem = refs[-3:]
    total = keep_ref[...].astype(jnp.float32) + taken_ref[...].astype(jnp.float32)
    sum_ref[...] = total.astype(sum_ref.dtype)
    store = pltpu.make_async_copy(sum_ref, out_hbm.at[:, pl.ds(at, keep_ref.shape[1])], sem)
    store.start()
    store.wait()


def pair_sum(keep, taken, at, d_local, into=None):
    vmem, hbm = (pl.BlockSpec(memory_space=m) for m in (pltpu.VMEM, pltpu.HBM))
    whole = [] if into is None else [into]
    return pl.pallas_call(
        functools.partial(pair_kernel, at),
        out_shape=jax.ShapeDtypeStruct((keep.shape[0], d_local), keep.dtype),
        in_specs=[vmem] * 2 + [hbm] * len(whole),
        out_specs=hbm,
        input_output_aliases={2: 0} if whole else {},
        scratch_shapes=[pltpu.VMEM(keep.shape, keep.dtype), pltpu.SemaphoreType.DMA(())],
        name="pairsum",
        cost_estimate=pl.CostEstimate(
            flops=keep.size, bytes_accessed=6 * keep.size, transcendentals=0
        ),
        compiler_params=pltpu.CompilerParams(vmem_limit_bytes=8 * MIB),
    )(keep, taken, *whole)


def wgrad_kernel(n_row, n_cut, scaling, *refs):
    q_refs, refs = refs[: n_row * n_cut], refs[n_row * n_cut :]
    mine_ref, other_ref, out_hbm, x_ref, q_ref, held, sems = refs
    tr = q_refs[0].shape[0]
    half = tr // CORES
    slots, block, _ = held.shape
    core = lax.rem(lax.axis_index("col"), CORES)
    for c in range(CORES):

        @pl.when(core == c)
        def _():
            for j in range(n_row):
                at = pl.ds(row_start(j, n_row, half), half)
                for k in range(CORES):
                    source = mine_ref if k == c else other_ref
                    to = j * tr + k * half
                    x_ref[to : to + half, :] = source[at, :]

    for j in range(n_row):
        start = 0
        for i in range(n_cut):
            part = q_refs[i * n_row + j]
            end = start + part.shape[1]
            q_ref[j * tr : (j + 1) * tr, start:end] = part[...]
            start = end

    f_local = out_hbm.shape[1]
    cuts = (0, f_local // (2 * LANES) * LANES, f_local)
    sides = [slice(*side) for side in zip(cuts, cuts[1:], strict=False)]

    def store(step, side):
        slot = lax.rem(step, slots)
        rows = pl.ds(pl.multiple_of(step * block, block), block)
        return pltpu.make_async_copy(
            held.at[slot, :, sides[side]], out_hbm.at[rows, sides[side]], sems.at[slot, side]
        )

    steps = out_hbm.shape[0] // block

    @pl.loop(0, steps)
    def _(step):
        rows = pl.ds(pl.multiple_of(step * block, block), block)
        for side in range(len(sides)):

            @pl.when(step >= slots)
            def _():
                store(step - slots, side).wait()

            held[lax.rem(step, slots), :, sides[side]] = scaling * lax.dot_general(
                x_ref[:, rows],
                q_ref[:, sides[side]],
                (((0,), (0,)), ((), ())),
                preferred_element_type=jnp.float32,
            )
            store(step, side).start()

    for step in range(max(steps - slots, 0), steps):
        for side in range(len(sides)):
            store(step, side).wait()


def wgrad(q_cuts, x_mine, x_other, scaling):
    n_cut, n_row = len(q_cuts), len(q_cuts[0])
    tr = q_cuts[0][0].shape[0]
    f_local = sum(parts[0].shape[1] for parts in q_cuts)
    tokens, d_local = tr * n_row, x_mine.shape[1]
    block = largest_block(d_local, 256)
    slots = min(3, d_local // block)
    vmem = pl.BlockSpec(memory_space=pltpu.VMEM)
    return pl.pallas_call(
        functools.partial(wgrad_kernel, n_row, n_cut, scaling),
        out_shape=jax.ShapeDtypeStruct((d_local, f_local), jnp.float32),
        in_specs=[vmem] * (n_row * n_cut + 2),
        out_specs=pl.BlockSpec(memory_space=pltpu.HBM),
        scratch_shapes=[
            pltpu.VMEM((tokens, d_local), jnp.bfloat16),
            pltpu.VMEM((tokens, f_local), jnp.bfloat16),
            pltpu.VMEM((slots, block, f_local), jnp.float32),
            pltpu.SemaphoreType.DMA((slots, 2)),
        ],
        name="wgrad",
        cost_estimate=pl.CostEstimate(
            flops=2 * tokens * d_local * f_local,
            bytes_accessed=4 * d_local * f_local,
            transcendentals=0,
        ),
        compiler_params=pltpu.CompilerParams(vmem_limit_bytes=VMEM_WGRAD * MIB),
    )(*[part for parts in q_cuts for part in parts], x_mine, x_other)


def shards(activations, up_weight, out_grad, round_seed, counter_base):
    n_row, n_col = lax.axis_size("row"), lax.axis_size("col")
    n_chip = n_col // CORES
    assert n_col % (CORES * n_row) == 0
    per_col, d_local = activations.shape
    tokens = per_col * n_col
    chips = [[chip * CORES + c for chip in range(n_chip)] for c in range(CORES)]
    swap = [(i, i ^ 1) for i in range(n_col)]

    f_local = out_grad.shape[1]
    middle = -(-f_local // (2 * LANES)) * LANES
    cuts = (0, middle, f_local)
    block = project_block(d_local)
    steps = d_local // block
    d_head, d_cut = block * max(1, steps // 4), block * (3 * steps // 4)
    shifts = [[(i, (i + j) % n_row) for i in range(n_row)] for j in range(1, n_row)]
    owns, copies, head = stochastic_round(
        out_grad, counter_base, round_seed, activations, up_weight, cuts, n_chip
    )
    q_a = [owns[0]] + [lax.ppermute(owns[0], "row", shift) for shift in shifts]
    q_b = [owns[1]] + [lax.ppermute(owns[1], "row", shift) for shift in shifts]
    x_mine = lax.all_to_all(copies, "col", 0, 0, axis_index_groups=chips)
    x_mine = x_mine.reshape(n_chip * per_col, d_local)
    x_other = lax.ppermute(x_mine, "col", swap)
    total, head = project(
        q_a, up_weight, None, head, (0, d_local), 0, False, ((0, d_head), (middle, f_local))
    )
    keep_a, give_a, head = project(
        q_b, up_weight, total, head, (0, d_cut), middle, True, ((d_cut, d_local), (middle, f_local))
    )
    keep_b, give_b = project(q_b, up_weight, total, head, (d_cut, d_local), middle, True)
    taken_a = lax.ppermute(give_a, "col", swap)
    taken_b = lax.ppermute(give_b, "col", swap)
    pair = pair_sum(keep_a, taken_a, 0, d_local)
    pair = pair_sum(keep_b, taken_b, d_cut, d_local, pair)
    pair = pair.reshape(n_chip, per_col, d_local)
    shares = lax.all_to_all(pair, "col", 0, 0, axis_index_groups=chips)
    weight_grad = wgrad((q_a, q_b), x_mine, x_other, tokens ** (-0.5))
    input_grad = jnp.sum(shares.astype(jnp.float32), axis=0)
    return weight_grad, input_grad.astype(jnp.bfloat16)


def solution(mesh):
    placed = (P("col", "row"), P("row", "col"), P("row", "col"), P(), P("row"))
    return jax.shard_map(
        shards,
        mesh=mesh,
        in_specs=placed,
        out_specs=(P("row", "col"), P("col", "row")),
        check_vma=False,
    )
```

```python
import functools

import jax
import jax.numpy as jnp
from jax import lax
from jax.experimental import pallas as pl
from jax.experimental.pallas import tpu as pltpu
from jax.sharding import PartitionSpec as P


CORES = 2
LANES = 256
MIB = 2**20


def round_kernel(per_col, cuts, seed_ref, base_hbm, grad_hbm, x_hbm, w_hbm, *refs):
    n_cut = len(cuts) - 1
    out_refs, refs = refs[:n_cut], refs[n_cut:]
    copies_hbm, head_ref, base_ref, grad_ref, x_ref, sems, copy_sems = refs
    loads = [
        pltpu.make_async_copy(x_hbm, x_ref, sems.at[0]),
        pltpu.make_async_copy(base_hbm, base_ref, sems.at[1]),
    ] + [
        pltpu.make_async_copy(
            grad_hbm.at[:, cut:end], grad_ref.at[:, cut:end], sems.at[2 + i]
        )
        for i, (cut, end) in enumerate(zip(cuts, cuts[1:], strict=False))
    ]
    loads.append(
        pltpu.make_async_copy(
            w_hbm.at[: head_ref.shape[0], : head_ref.shape[1]], head_ref, sems.at[1 + len(cuts)]
        )
    )
    for load in loads:
        load.start()
    stores = [
        pltpu.make_async_copy(x_ref, copies_hbm.at[i], copy_sems.at[i])
        for i in range(copies_hbm.shape[0])
    ]
    loads[1].wait()
    rows, f_local = grad_ref.shape
    shape = (rows, rows)
    diagonal = lax.broadcasted_iota(jnp.int32, shape, 0) == lax.broadcasted_iota(
        jnp.int32, shape, 1
    )
    base = jnp.where(diagonal, jnp.broadcast_to(base_ref[...], shape), 0)
    base = jnp.sum(base, axis=1, keepdims=True)
    col_first = lax.axis_index("col") * f_local
    offset = seed_ref[0] * jnp.int32(1013904223)
    loads[0].wait()
    for store in stores:
        store.start()
    for out_ref, load, cut, end in zip(out_refs, loads[2:-1], cuts, cuts[1:], strict=False):
        load.wait()
        width = largest_block(end - cut, 256)
        for start in range(cut, end, width):
            columns = lax.broadcasted_iota(jnp.int32, (rows, width), 1)
            counter = base + (columns + (col_first + start))
            mixed = counter * jnp.int32(747796405) + offset
            mixed = mixed ^ (mixed >> 15)
            mixed = mixed * jnp.int32(277803737)
            mixed = mixed ^ (mixed >> 16)
            level = (mixed & 255).astype(jnp.float32)
            grad = grad_ref[:, start : start + width].astype(jnp.float32)
            done = jnp.floor(grad * 4.0 + (level + 0.5) / 256.0) / 4.0
            pieces = [done[i : i + per_col] for i in range(0, rows, per_col)]
            pieces = [p for c in range(CORES) for p in pieces[c::CORES]]
            at = slice(start - cut, start - cut + width)
            out_ref[:, at] = jnp.concatenate(pieces).astype(out_ref.dtype)
    for store in stores:
        store.wait()
    loads[-1].wait()


def stochastic_round(
    grad, counter_base, round_seed, activations, up_weight, cuts, n_chip
):
    per_col, d_local = activations.shape
    rows = grad.shape[0]
    vmem = pl.BlockSpec(memory_space=pltpu.VMEM)
    hbm = pl.BlockSpec(memory_space=pltpu.HBM)
    *parts, copies, head = pl.pallas_call(
        functools.partial(round_kernel, per_col, cuts),
        out_shape=[
            jax.ShapeDtypeStruct((rows, end - cut), jnp.bfloat16)
            for cut, end in zip(cuts, cuts[1:], strict=False)
        ]
        + [
            pltpu.HBM((n_chip, per_col, d_local), activations.dtype),
            jax.ShapeDtypeStruct((project_block(d_local), cuts[1]), up_weight.dtype),
        ],
        in_specs=[pl.BlockSpec(memory_space=pltpu.SMEM)] + [hbm] * 4,
        out_specs=[vmem] * (len(cuts) - 1) + [hbm, vmem],
        scratch_shapes=[
            pltpu.VMEM((1, rows), jnp.int32),
            pltpu.VMEM(grad.shape, grad.dtype),
            pltpu.VMEM(activations.shape, activations.dtype),
            pltpu.SemaphoreType.DMA((2 + len(cuts),)),
            pltpu.SemaphoreType.DMA((n_chip,)),
        ],
        name="quantize",
        cost_estimate=pl.CostEstimate(
            flops=16 * grad.size, bytes_accessed=4 * grad.size, transcendentals=0
        ),
        compiler_params=pltpu.CompilerParams(vmem_limit_bytes=8 * MIB),
    )(round_seed, *in_hbm(counter_base[None, :], grad, activations, up_weight))
    return parts, copies, head


def in_hbm(*arrays):
    return [pltpu.with_memory_space_constraint(a, pltpu.HBM) for a in arrays]


def largest_block(length, most):
    return next(b for b in range(min(most, length), 0, -1) if length % b == 0)


def row_start(j, rows, size):
    owner = lax.rem(lax.axis_index("row") - j + rows, rows)
    return pl.multiple_of(owner * size, size)


def project_block(d_local):
    return largest_block(d_local, 512)


def project_kernel(n_row, first, final, d_from, f_from, next_at, block, *refs):
    q_refs, refs = refs[:n_row], list(refs[n_row:])
    sum_ref = None if first else refs.pop(0)
    head_ref, w_hbm = refs.pop(0), refs.pop(0)
    out_refs = [refs.pop(0) for _ in range(CORES if final else 1)]
    ahead_ref = None if next_at is None else refs.pop(0)
    w_ref, sems = refs.pop(0), refs.pop(0)
    head = head_ref.shape[0] // block
    tr, f_len = q_refs[0].shape
    half = tr // CORES
    core = lax.rem(lax.axis_index("col"), CORES)
    steps = out_refs[0].shape[1 if final else 0] // block

    def rows_of(step, start=0):
        return pl.ds(pl.multiple_of(step * block + start, block), block)

    def fetch(step):
        source = w_hbm.at[rows_of(step, d_from), pl.ds(f_from, f_len)]
        return pltpu.make_async_copy(source, w_ref.at[rows_of(step - head), :], sems.at[step])

    def multiply(step, weight_ref, weight_step):
        at_d = rows_of(step)
        part = lax.dot_general(
            weight_ref[rows_of(weight_step), :],
            jnp.concatenate([q_ref[...] for q_ref in q_refs], axis=0),
            (((1,), (1,)), ((), ())),
            preferred_element_type=jnp.float32,
        )
        if sum_ref is not None:
            part = part + sum_ref[rows_of(step, d_from), :]
        if not final:
            out_refs[0][at_d, :] = part
            return
        turned_ref = refs[0]
        turned_ref[...] = part.astype(jnp.bfloat16).T
        for j in range(n_row):
            at = pl.ds(row_start(j, n_row, half), half)
            for out_ref, c in zip(out_refs, (core, 1 - core), strict=True):
                source = pl.multiple_of(j * tr + c * half, half)
                out_ref[at, at_d] = turned_ref[pl.ds(source, half), :]

    for step in range(head, steps):
        fetch(step).start()
    if ahead_ref is not None:
        d_next, f_next = next_at
        n_d, n_f = ahead_ref.shape
        source = w_hbm.at[d_next : d_next + n_d, f_next : f_next + n_f]
        ahead = pltpu.make_async_copy(source, ahead_ref, sems.at[steps])
        ahead.start()

    @pl.loop(0, head)
    def _(step):
        multiply(step, head_ref, step)

    if head < steps:

        @pl.loop(head, steps)
        def _(step):
            fetch(step).wait()
            multiply(step, w_ref, step - head)

    if ahead_ref is not None:
        ahead.wait()


def project(q_parts, up_weight, total, head, d_cut, f_from, final, following=None):
    n_row = len(q_parts)
    tr, f_len = q_parts[0].shape
    tokens = tr * n_row
    d_from, d_to = d_cut
    size = d_to - d_from
    block = project_block(up_weight.shape[0])
    steps = size // block
    vmem = pl.BlockSpec(memory_space=pltpu.VMEM)
    scratch = [
        pltpu.VMEM((max(size - head.shape[0], block), f_len), up_weight.dtype),
        pltpu.SemaphoreType.DMA((steps + 1,)),
    ]
    if final:
        scratch.append(pltpu.VMEM((tokens, block), jnp.bfloat16))
        out = [jax.ShapeDtypeStruct((tokens // CORES, size), jnp.bfloat16)] * CORES
    else:
        out = [jax.ShapeDtypeStruct((size, tokens), jnp.float32)]
    next_at = None
    if following is not None:
        next_at = tuple(start for start, _ in following)
        shape = tuple(end - start for start, end in following)
        out.append(jax.ShapeDtypeStruct(shape, up_weight.dtype))
    before = [] if total is None else [total]
    return pl.pallas_call(
        functools.partial(
            project_kernel, n_row, total is None, final, d_from, f_from, next_at, block
        ),
        out_shape=out,
        in_specs=[vmem] * (n_row + len(before) + 1) + [pl.BlockSpec(memory_space=pltpu.HBM)],
        out_specs=[vmem] * len(out),
        scratch_shapes=scratch,
        name="project",
        cost_estimate=pl.CostEstimate(
            flops=2 * tokens * size * f_len,
            bytes_accessed=2 * size * f_len,
            transcendentals=0,
        ),
        compiler_params=pltpu.CompilerParams(vmem_limit_bytes=VMEM_PROJECT * MIB),
    )(*q_parts, *before, head, *in_hbm(up_weight))


VMEM_PROJECT = 28
VMEM_WGRAD = 32


def pair_kernel(at, keep_ref, taken_ref, *refs):
    out_hbm, sum_ref, sem = refs[-3:]
    total = keep_ref[...].astype(jnp.float32) + taken_ref[...].astype(jnp.float32)
    sum_ref[...] = total.astype(sum_ref.dtype)
    store = pltpu.make_async_copy(sum_ref, out_hbm.at[:, pl.ds(at, keep_ref.shape[1])], sem)
    store.start()
    store.wait()


def pair_sum(keep, taken, at, d_local, into=None):
    vmem, hbm = (pl.BlockSpec(memory_space=m) for m in (pltpu.VMEM, pltpu.HBM))
    whole = [] if into is None else [into]
    return pl.pallas_call(
        functools.partial(pair_kernel, at),
        out_shape=jax.ShapeDtypeStruct((keep.shape[0], d_local), keep.dtype),
        in_specs=[vmem] * 2 + [hbm] * len(whole),
        out_specs=hbm,
        input_output_aliases={2: 0} if whole else {},
        scratch_shapes=[pltpu.VMEM(keep.shape, keep.dtype), pltpu.SemaphoreType.DMA(())],
        name="pairsum",
        cost_estimate=pl.CostEstimate(
            flops=keep.size, bytes_accessed=6 * keep.size, transcendentals=0
        ),
        compiler_params=pltpu.CompilerParams(vmem_limit_bytes=8 * MIB),
    )(keep, taken, *whole)


def wgrad_kernel(n_row, n_cut, scaling, *refs):
    q_refs, refs = refs[: n_row * n_cut], refs[n_row * n_cut :]
    mine_ref, other_ref, out_hbm, x_ref, q_ref, held, sems = refs
    tr = q_refs[0].shape[0]
    half = tr // CORES
    slots, block, _ = held.shape
    core = lax.rem(lax.axis_index("col"), CORES)
    for j in range(n_row):
        start = 0
        for i in range(n_cut):
            part = q_refs[i * n_row + j]
            end = start + part.shape[1]
            q_ref[j * tr : (j + 1) * tr, start:end] = part[...]
            start = end

    f_local = out_hbm.shape[1]
    count = sems.shape[1]
    cuts = [i * (f_local // LANES) // count * LANES for i in range(count)] + [f_local]
    sides = [slice(*side) for side in zip(cuts, cuts[1:], strict=False)]

    def store(step, side):
        slot = lax.rem(step, slots)
        rows = pl.ds(pl.multiple_of(step * block, block), block)
        return pltpu.make_async_copy(
            held.at[slot, :, sides[side]], out_hbm.at[rows, sides[side]], sems.at[slot, side]
        )

    steps = out_hbm.shape[0] // block

    @pl.loop(0, steps)
    def _(step):
        rows = pl.ds(pl.multiple_of(step * block, block), block)
        for c in range(CORES):

            @pl.when(core == c)
            def _():
                for j in range(n_row):
                    at = pl.ds(row_start(j, n_row, half), half)
                    for k in range(CORES):
                        source = mine_ref if k == c else other_ref
                        to = j * tr + k * half
                        x_ref[to : to + half, :] = source[at, rows]

        for side in range(len(sides)):

            @pl.when(step >= slots)
            def _():
                store(step - slots, side).wait()

            held[lax.rem(step, slots), :, sides[side]] = scaling * lax.dot_general(
                x_ref[...],
                q_ref[:, sides[side]],
                (((0,), (0,)), ((), ())),
                preferred_element_type=jnp.float32,
            )
            store(step, side).start()

    for step in range(max(steps - slots, 0), steps):
        for side in range(len(sides)):
            store(step, side).wait()


def wgrad(q_cuts, x_mine, x_other, scaling):
    n_cut, n_row = len(q_cuts), len(q_cuts[0])
    tr = q_cuts[0][0].shape[0]
    f_local = sum(parts[0].shape[1] for parts in q_cuts)
    tokens, d_local = tr * n_row, x_mine.shape[1]
    block = largest_block(d_local, 256)
    slots = min(3, d_local // block)
    vmem = pl.BlockSpec(memory_space=pltpu.VMEM)
    return pl.pallas_call(
        functools.partial(wgrad_kernel, n_row, n_cut, scaling),
        out_shape=jax.ShapeDtypeStruct((d_local, f_local), jnp.float32),
        in_specs=[vmem] * (n_row * n_cut + 2),
        out_specs=pl.BlockSpec(memory_space=pltpu.HBM),
        scratch_shapes=[
            pltpu.VMEM((tokens, block), jnp.bfloat16),
            pltpu.VMEM((tokens, f_local), jnp.bfloat16),
            pltpu.VMEM((slots, block, f_local), jnp.float32),
            pltpu.SemaphoreType.DMA((slots, 2)),
        ],
        name="wgrad",
        cost_estimate=pl.CostEstimate(
            flops=2 * tokens * d_local * f_local,
            bytes_accessed=4 * d_local * f_local,
            transcendentals=0,
        ),
        compiler_params=pltpu.CompilerParams(vmem_limit_bytes=VMEM_WGRAD * MIB),
    )(*[part for parts in q_cuts for part in parts], x_mine, x_other)


def shards(activations, up_weight, out_grad, round_seed, counter_base):
    n_row, n_col = lax.axis_size("row"), lax.axis_size("col")
    n_chip = n_col // CORES
    assert n_col % (CORES * n_row) == 0
    per_col, d_local = activations.shape
    tokens = per_col * n_col
    chips = [[chip * CORES + c for chip in range(n_chip)] for c in range(CORES)]
    swap = [(i, i ^ 1) for i in range(n_col)]

    f_local = out_grad.shape[1]
    middle = -(-f_local // (2 * LANES)) * LANES
    cuts = (0, middle, f_local)
    block = project_block(d_local)
    steps = d_local // block
    d_head, d_cut = block * max(1, steps // 4), block * (3 * steps // 4)
    shifts = [[(i, (i + j) % n_row) for i in range(n_row)] for j in range(1, n_row)]
    owns, copies, head = stochastic_round(
        out_grad, counter_base, round_seed, activations, up_weight, cuts, n_chip
    )
    q_a = [owns[0]] + [lax.ppermute(owns[0], "row", shift) for shift in shifts]
    q_b = [owns[1]] + [lax.ppermute(owns[1], "row", shift) for shift in shifts]
    x_mine = lax.all_to_all(copies, "col", 0, 0, axis_index_groups=chips)
    x_mine = x_mine.reshape(n_chip * per_col, d_local)
    x_other = lax.ppermute(x_mine, "col", swap)
    total, head = project(
        q_a, up_weight, None, head, (0, d_local), 0, False, ((0, d_head), (middle, f_local))
    )
    keep_a, give_a, head = project(
        q_b, up_weight, total, head, (0, d_cut), middle, True, ((d_cut, d_local), (middle, f_local))
    )
    keep_b, give_b = project(q_b, up_weight, total, head, (d_cut, d_local), middle, True)
    taken_a = lax.ppermute(give_a, "col", swap)
    taken_b = lax.ppermute(give_b, "col", swap)
    pair = pair_sum(keep_a, taken_a, 0, d_local)
    pair = pair_sum(keep_b, taken_b, d_cut, d_local, pair)
    pair = pair.reshape(n_chip, per_col, d_local)
    shares = lax.all_to_all(pair, "col", 0, 0, axis_index_groups=chips)
    weight_grad = wgrad((q_a, q_b), x_mine, x_other, tokens ** (-0.5))
    input_grad = jnp.sum(shares.astype(jnp.float32), axis=0)
    return weight_grad, input_grad.astype(jnp.bfloat16)


def solution(mesh):
    placed = (P("col", "row"), P("row", "col"), P("row", "col"), P(), P("row"))
    return jax.shard_map(
        shards,
        mesh=mesh,
        in_specs=placed,
        out_specs=(P("row", "col"), P("col", "row")),
        check_vma=False,
    )
```
